128 devices in a mesh: freq: 8 (over x, core), tile: 16 (over z, y).
Axes of the slice: x: 4, y: 4, z: 4, core: 2. Of those that a mesh axis runs over, the one named last changes fastest.
Arguments:
- virtual_source_trace: bfloat16 [512, 4, 8400], P(('freq', 'tile')), may hold values from -6 to 6
- v_bases: bfloat16 [8, 192, 120, 2, 32, 70], P('freq', 'tile'), may hold values from -0.75 to 0.75
- u_bases: bfloat16 [8, 192, 120, 2, 32, 70], P('freq', 'tile'), may hold values from -0.09375 to 0.09375
- ranks: int32 [8, 192, 120], P('freq', 'tile'), may hold values from 16 to 32, as said below
- freq_bin: int32 [8], replicated, may hold values from 1 to 255
- slab_order: int32 [128], replicated, may hold values from 0 to 127, each once
Outputs:
- redatumed: bfloat16 [512, 4, 13440], P(('freq', 'tile'))
The draws below stay inside these ranges and needn't reach their ends.
Inputs may be any that keep to these rules, and one draw needn't show every extreme that they name: `ranks`: every rank is 16 or 32.
All inputs are finite; a program needn't handle non-finite values.
Results may differ from the reference program's by a relative error of at most 0.008.
Values may be sent and summed in bfloat16 or wider, within the bound.
A program may use at most 192 MiB of HBM per device.

```python
import math
import jax
import jax.numpy as jnp
from jax import lax

TILE_EXTENT = 70
TILE_ROWS = 192
TILE_COLUMNS = 120
RBLOCK = 16
VIRTUAL_SOURCES = 4
TIME_DEV = 4
RMAX = 32
SOURCE_COUNT = 8400
WINDOW_FREQS = 8
TIME_SAMPLES = 512
DEVICES = 128


def draw_ranks(key, part):
    level_key = jax.random.fold_in(key, 11)
    tile_key = jax.random.fold_in(key, 23)
    levels = jax.random.randint(level_key, (WINDOW_FREQS, 1, 1), 0, 5)
    tickets = jax.random.randint(tile_key, (WINDOW_FREQS, TILE_ROWS, TILE_COLUMNS), 0, 4)
    return (RBLOCK + RBLOCK * (tickets < levels).astype(jnp.int32)).astype(jnp.int32)


def with_ends(entries, stream_key, smallest, largest):
    dims = entries.shape
    place = [jax.random.randint(jax.random.fold_in(stream_key, axis), (), 0, dims[axis]) for axis in range(len(dims))]
    entries = entries.at[tuple(place)].set(smallest)
    longest = dims.index(max(dims))
    place[longest] = (place[longest] + 1) % dims[longest]
    return entries.at[tuple(place)].set(largest)


def block_scale(rng, extent, pieces, smallest, top_value):
    def one(dim, shards_of):
        heights = jax.random.uniform(jax.random.fold_in(jax.random.fold_in(rng, 6), dim), (shards_of,), jnp.float32, smallest / len(pieces), top_value / len(pieces))
        return jnp.repeat(jnp.exp(heights), extent[dim] // shards_of).reshape((-1,) + (1,) * (len(extent) - dim - 1))

    factor_of = one(*pieces[0])
    for cut in pieces[1:]:
        factor_of = factor_of * one(*cut)
    return factor_of


def bell_draw(stream_key, extent, width, reach, cuts=(), kind=jnp.bfloat16):
    drawn = jax.random.normal(stream_key, extent, jnp.float32) * width
    if len(cuts) > 0:
        drawn = block_scale(stream_key, extent, cuts, -0.22, 0.18) * drawn
    return jnp.clip(drawn, min=-reach, max=reach).astype(kind)


def setup_inputs(seed: int = 0) -> dict:
    key_list = jax.random.split(jax.random.key(seed), 7)
    virtual_source_trace = bell_draw(key_list[0], (TIME_SAMPLES, VIRTUAL_SOURCES, SOURCE_COUNT), 1.0, 6.0, ((0, 128),))
    v_bases = bell_draw(key_list[1], (WINDOW_FREQS, TILE_ROWS, TILE_COLUMNS, 2, RMAX, TILE_EXTENT), TILE_EXTENT ** -0.5, 0.75, ((0, 8), (1, 16)))
    u_bases = bell_draw(key_list[2], (WINDOW_FREQS, TILE_ROWS, TILE_COLUMNS, 2, RMAX, TILE_EXTENT), (RMAX * TILE_COLUMNS) ** -0.5, 0.09375, ((0, 8), (1, 16)))
    ranks = draw_ranks(jax.random.fold_in(key_list[6], 71), 0)
    freq_bin = with_ends(jax.random.randint(key_list[4], (WINDOW_FREQS,), 1, TIME_SAMPLES // 2), jax.random.fold_in(key_list[4], 1), 1, (TIME_SAMPLES // 2) - 1).astype(jnp.int32)
    slab_order = jax.random.permutation(key_list[5], DEVICES).astype(jnp.int32)
    return dict(virtual_source_trace=virtual_source_trace, v_bases=v_bases, u_bases=u_bases, ranks=ranks, freq_bin=freq_bin, slab_order=slab_order)


def angles_of(freq_bin, times, total):
    products = freq_bin[:, None] * times[None, :] % total
    return products.astype(jnp.float32) * (2.0 * math.pi / total)

def rounded(values):
    return lax.optimization_barrier(values.astype(jnp.bfloat16)).astype(jnp.float32)

def apply_kernel(operands):
    v_part, u_part, rank_part, spec_part = operands
    basis_re = v_part[:, :, 0].astype(jnp.float32)
    basis_im = v_part[:, :, 1].astype(jnp.float32)
    left_re = u_part[:, :, 0].astype(jnp.float32)
    left_im = u_part[:, :, 1].astype(jnp.float32)
    spec_re = spec_part[0].astype(jnp.float32)
    spec_im = spec_part[1].astype(jnp.float32)

    def project(factor_basis, spec):
        return jnp.einsum('ijrp,vjp->ijrv', factor_basis, spec)
    coef_re = project(basis_re, spec_re) - project(basis_im, spec_im)
    coef_im = project(basis_re, spec_im) + project(basis_im, spec_re)
    rank_mask = (jnp.arange(RMAX, dtype=jnp.int32)[None, None, :] < rank_part[:, :, None]).astype(jnp.float32)[..., None]
    coef_re = rounded(coef_re * rank_mask)
    coef_im = rounded(coef_im * rank_mask)

    def expand(factor_basis, factor_weight):
        return jnp.einsum('debs,debm->mds', factor_basis, factor_weight).reshape(VIRTUAL_SOURCES, TILE_ROWS * TILE_EXTENT)
    out_re = expand(left_re, coef_re) - expand(left_im, coef_im)
    out_im = expand(left_re, coef_im) + expand(left_im, coef_re)
    return jnp.stack([out_re, out_im])

def reference(virtual_source_trace, v_bases, u_bases, ranks, freq_bin, slab_order):
    times = (slab_order[:, None] * TIME_DEV + jnp.arange(TIME_DEV, dtype=jnp.int32)[None, :]).reshape(TIME_SAMPLES).astype(jnp.int32)
    angles = angles_of(freq_bin.astype(jnp.int32), times, TIME_SAMPLES)
    forward = jnp.stack([jnp.cos(angles), -jnp.sin(angles)], axis=1) / math.sqrt(TIME_SAMPLES)
    frequency_spectra = jnp.einsum('fct,tvs->fcvs', forward, virtual_source_trace.astype(jnp.float32), precision=lax.Precision.HIGHEST)
    frequency_spectra = frequency_spectra.astype(jnp.bfloat16).reshape(WINDOW_FREQS, 2, VIRTUAL_SOURCES, TILE_COLUMNS, TILE_EXTENT)
    received = lax.map(apply_kernel, (v_bases, u_bases, ranks, frequency_spectra))
    inverse = jnp.stack([jnp.cos(angles.T), -jnp.sin(angles.T)], axis=2) / math.sqrt(WINDOW_FREQS)
    redatumed = jnp.einsum('tfc,fcvn->tvn', inverse, received, precision=lax.Precision.HIGHEST)
    return redatumed.astype(jnp.bfloat16)
```

```python
import functools
import math

import jax
import jax.numpy as jnp
from jax import lax
from jax.experimental import pallas as pl
from jax.experimental.pallas import tpu as pltpu
from jax.sharding import PartitionSpec as P

F32, BF16 = jnp.float32, jnp.bfloat16
MESH = pl.DeviceIdType.MESH
EXT = 70
COLS = 120
RANK = 32
NV = 4
NT = 4
ROWS = 12
NTILE = 16
NFREQ = 8
CHUNK = 5
OUT = 13440
NT_DIMS = (((1,), (1,)), ((), ()))


def chunk_start(k):
    return (k * (EXT - CHUNK) + 7) // (NTILE - 1)


def split(x):
    hi = x.astype(BF16)
    return hi, (x - hi.astype(F32)).astype(BF16)


def tree(xs):
    while len(xs) > 1:
        xs = [a + b for a, b in zip(xs[::2], xs[1::2])] + ([xs[-1]] if len(xs) % 2 else [])
    return xs[0]


def peers():
    g, k = lax.axis_index("freq"), lax.axis_index("tile")
    over_tile = [(d, lax.rem(k + d, NTILE)) for d in range(1, NTILE)]
    over_freq = [(d, lax.rem(g + d, NFREQ)) for d in range(1, NFREQ)]
    return g, k, over_tile, over_freq


def enter(over_tile, over_freq):
    barrier = pltpu.get_barrier_semaphore()
    for _, kk in over_tile:
        pl.semaphore_signal(barrier, inc=1, device_id={"tile": kk}, device_id_type=MESH)
    for _, f in over_freq:
        pl.semaphore_signal(barrier, inc=1, device_id={"freq": f}, device_id_type=MESH)
    pl.semaphore_wait(barrier, NTILE + NFREQ - 2)


def remote(src, dst, send, recv, axis, to):
    return pltpu.make_async_remote_copy(
        src_ref=src, dst_ref=dst, send_sem=send, recv_sem=recv, device_id={axis: to}, device_id_type=MESH
    )


def spectra_kernel(t_ref, w_ref, x_ref, a1, s2, b2, s3, b3, own, ss1, rs1, ss2, rs2, ss3, rs3):
    g, k, over_tile, over_freq = peers()
    enter(over_tile, over_freq)
    mine = pltpu.make_async_copy(t_ref.at[pl.ds(chunk_start(k), CHUNK)], a1.at[k], own)
    mine.start()
    sends = []
    for _, kk in over_tile:
        c = remote(t_ref.at[pl.ds(chunk_start(kk), CHUNK)], a1.at[k], ss1.at[kk], rs1.at[k], "tile", kk)
        c.start()
        sends.append(c)
    mine.wait()
    for _, kk in over_tile:
        remote(t_ref.at[pl.ds(0, CHUNK)], a1.at[kk], ss1.at[kk], rs1.at[kk], "tile", kk).wait_recv()
    for p in range(CHUNK):
        data = a1[:, p].reshape(NTILE * 16, 128)
        both = jnp.dot(w_ref[...], data, preferred_element_type=F32)
        s2[:, p] = (both[:64] + both[64:]).reshape(NFREQ, 8, 128).astype(BF16)
    for _, f in over_freq:
        c = remote(s2.at[f], b2.at[g], ss2.at[f], rs2.at[g], "freq", f)
        c.start()
        sends.append(c)
    total = s2[g].astype(F32)
    for _, f in over_freq:
        remote(s2.at[f], b2.at[f], ss2.at[f], rs2.at[f], "freq", f).wait_recv()
        total = total + b2[f].astype(F32)
    s3[...] = total.astype(BF16)
    for _, kk in over_tile:
        c = remote(s3, b3.at[k], ss3.at[kk], rs3.at[k], "tile", kk)
        c.start()
        sends.append(c)
    b3[k] = s3[...]
    for _, kk in over_tile:
        remote(s3, b3.at[kk], ss3.at[kk], rs3.at[kk], "tile", kk).wait_recv()
    for kk in range(NTILE):
        for p in range(CHUNK):
            x = b3[kk, p].astype(F32)
            xr, xi = x[0:4], x[4:8]
            x_ref[chunk_start(kk) + p] = jnp.concatenate([xr, xi - xr, xr + xi, xr], axis=0)
    for c in sends:
        c.wait_send()


def spectra(t, w):
    vmem = pl.BlockSpec(memory_space=pltpu.VMEM)
    dma = pltpu.SemaphoreType.DMA
    return pl.pallas_call(
        spectra_kernel,
        out_shape=jax.ShapeDtypeStruct((EXT, 16, 128), F32),
        in_specs=[vmem, vmem],
        out_specs=vmem,
        scratch_shapes=[
            pltpu.VMEM((NTILE, CHUNK, 16, 128), BF16),
            pltpu.VMEM((NFREQ, CHUNK, 8, 128), BF16),
            pltpu.VMEM((NFREQ, CHUNK, 8, 128), BF16),
            pltpu.VMEM((CHUNK, 8, 128), BF16),
            pltpu.VMEM((NTILE, CHUNK, 8, 128), BF16),
            dma,
            dma((NTILE,)), dma((NTILE,)), dma((NFREQ,)), dma((NFREQ,)), dma((NTILE,)), dma((NTILE,)),
        ],
        compiler_params=pltpu.CompilerParams(collective_id=0, has_side_effects=True),
    )(t, w)


def project(v_ref, x_ref, rank_row, ct):
    row = lax.broadcasted_iota(jnp.int32, (8, COLS), 0)
    for h in range(2):
        def body(p, acc):
            acc = list(acc)
            for a in range(2):
                r = 16 * h + 8 * a
                re = v_ref[0, 0, p, r:r + 8, :].astype(F32)
                im = v_ref[0, 1, p, r:r + 8, :].astype(F32)
                for n, b in enumerate((re + im, re, im)):
                    for v in range(NV):
                        m = 4 * n + v
                        acc[12 * a + m] += b * jnp.broadcast_to(x_ref[p, m:m + 1, :COLS], (8, COLS))
            return tuple(acc)

        acc = lax.fori_loop(0, EXT, body, (jnp.zeros((8, COLS), F32),) * 24, unroll=5)
        for a in range(2):
            keep = row + (16 * h + 8 * a) < rank_row
            for v in range(NV):
                k1, k2, k3 = (acc[12 * a + 4 * n + v] for n in range(3))
                re = jnp.where(keep, k1 - k3, 0.0).astype(BF16)
                im = jnp.where(keep, k1 + k2, 0.0).astype(BF16)
                n = 64 * a + 16 * v
                ct[h, n:n + 8, 0:COLS] = re
                ct[h, n:n + 8, 128:128 + COLS] = -im
                ct[h, n + 8:n + 16, 0:COLS] = im
                ct[h, n + 8:n + 16, 128:128 + COLS] = re


def expand(u_ref, ct, diag, step):
    lane = lax.broadcasted_iota(jnp.int32, (step * 16, 128), 1)
    low = lax.broadcasted_iota(jnp.int32, (step, 8, 128), 2) < 64
    for h in range(2):
        @pl.loop(0, EXT // step)
        def _(s):
            us = []
            for c in range(2):
                u = u_ref[0, c, pl.ds(s * step, step), 16 * h:16 * h + 16, :].reshape(step * 16, 128)
                us.append(jnp.where(lane < COLS, u, jnp.zeros_like(u)))
            z = lax.dot_general(jnp.concatenate(us, axis=1), ct[h], NT_DIMS, preferred_element_type=F32)
            z = z.reshape(step, 2, 8, 128)
            diag[h, pl.ds(s * step * 8, step * 8), :] = jnp.where(low, z[:, 0], z[:, 1]).reshape(step * 8, 128)


def collect(diag):
    lane = lax.broadcasted_iota(jnp.int32, (EXT, 128), 1) % 8
    halves = []
    for h in range(2):
        tot = diag[h, pl.ds(0, EXT, stride=8), :]
        for b in range(1, 8):
            tot = jnp.where(lane == b, diag[h, pl.ds(b, EXT, stride=8), :], tot)
        halves.append(tot)
    hi, lo = split(jnp.concatenate(halves, axis=1))
    rows = lax.broadcasted_iota(jnp.int32, (8, 256), 0)
    lanes = lax.broadcasted_iota(jnp.int32, (8, 256), 1)
    pick = ((lanes % 64) // 8 == (rows % 4) * 2 + rows // 4).astype(BF16)
    dot = functools.partial(lax.dot_general, dimension_numbers=NT_DIMS, preferred_element_type=F32)
    return dot(pick, hi) + dot(pick, lo)


def apply_kernel(step, rank_ref, x_ref, v_ref, u_ref, out_ref, ct, diag):
    @pl.when(pl.program_id(0) == 0)
    def _():
        ct[...] = jnp.zeros_like(ct)

    project(v_ref, x_ref, rank_ref[0], ct)
    expand(u_ref, ct, diag, step)
    out_ref[0] = jnp.zeros((8, 128), F32)
    out_ref[0, :, 0:EXT] = collect(diag)


def apply(ranks, x, v, u, step=14):
    return pl.pallas_call(
        functools.partial(apply_kernel, step),
        grid=(ROWS,),
        out_shape=jax.ShapeDtypeStruct((ROWS, 8, 128), F32),
        in_specs=[
            pl.BlockSpec((1, 1, COLS), lambda i: (i, 0, 0)),
            pl.BlockSpec((EXT, 16, 128), lambda i: (0, 0, 0)),
            pl.BlockSpec((1, 2, EXT, RANK, COLS), lambda i: (i, 0, 0, 0, 0)),
            pl.BlockSpec((1, 2, EXT, RANK, 128), lambda i: (i, 0, 0, 0, 0)),
        ],
        out_specs=pl.BlockSpec((1, 8, 128), lambda i: (i, 0, 0)),
        scratch_shapes=[pltpu.VMEM((2, 128, 256), BF16), pltpu.VMEM((2, EXT * 8, 128), F32)],
    )(ranks, x, v, u)


def output_kernel(r_ref, w_ref, out_ref, s1, b1, s2, b2, ss1, rs1, ss2, rs2):
    g, k, over_tile, over_freq = peers()
    lane = lax.broadcasted_iota(jnp.int32, (8, 128), 1)
    zero = jnp.zeros((8, 128), F32)
    tiles = [zero] * 8
    for i in range(ROWS):
        a, off = divmod(EXT * i, 128)
        piece = pltpu.roll(r_ref[i], off, 1) if off else r_ref[i]
        tiles[a] = tiles[a] + jnp.where(lane >= off, piece, 0.0)
        if off + EXT > 128:
            tiles[a + 1] = tiles[a + 1] + jnp.where(lane < off, piece, 0.0)
    off = lax.rem(k * (EXT * ROWS), 128)
    rolled = [zero] + [pltpu.roll(t, off, 1) for t in tiles]
    for a in range(8):
        s1[:, 128 * a:128 * a + 128] = jnp.where(lane >= off, rolled[a + 1], rolled[a]).astype(BF16)
    enter(over_tile, over_freq)
    sends = []
    for _, f in over_freq:
        c = remote(s1, b1.at[g], ss1.at[f], rs1.at[g], "freq", f)
        c.start()
        sends.append(c)
    b1[g] = s1[...]
    for _, f in over_freq:
        remote(s1, b1.at[f], ss1.at[f], rs1.at[f], "freq", f).wait_recv()
    r = b1[...].reshape(64, 1024)
    both = jnp.concatenate([r, r], axis=0)
    for c in range(4):
        lanes = slice(256 * c, 256 * c + 256)
        res = jnp.dot(w_ref[...], both[:, lanes], preferred_element_type=F32)
        s2[:, :, lanes] = res.reshape(NTILE, 16, 256).astype(BF16)
    for _, kk in over_tile:
        c = remote(s2.at[kk], b2.at[k], ss2.at[kk], rs2.at[k], "tile", kk)
        c.start()
        sends.append(c)
    b2[k] = s2[k]
    for _, kk in over_tile:
        remote(s2.at[kk], b2.at[kk], ss2.at[kk], rs2.at[kk], "tile", kk).wait_recv()
    parts = [[] for _ in range(OUT // 128)]
    for kk in range(NTILE):
        a, off = divmod(kk * EXT * ROWS, 128)
        for t in range((off + EXT * ROWS + 127) // 128):
            parts[a + t].append((kk, t))
    for m, ps in enumerate(parts):
        vals = [b2[kk, :, 128 * t:128 * t + 128] for kk, t in ps]
        out_ref[:, 128 * m:128 * m + 128] = tree(vals)
    for c in sends:
        c.wait_send()


def output(r, w):
    vmem = pl.BlockSpec(memory_space=pltpu.VMEM)
    dma = pltpu.SemaphoreType.DMA
    return pl.pallas_call(
        output_kernel,
        out_shape=jax.ShapeDtypeStruct((16, OUT), BF16),
        in_specs=[vmem, vmem],
        out_specs=vmem,
        scratch_shapes=[
            pltpu.VMEM((8, 1024), BF16),
            pltpu.VMEM((NFREQ, 8, 1024), BF16),
            pltpu.VMEM((NTILE, 16, 1024), BF16),
            pltpu.VMEM((NTILE, 16, 1024), BF16),
            dma((NFREQ,)), dma((NFREQ,)), dma((NTILE,)), dma((NTILE,)),
        ],
        compiler_params=pltpu.CompilerParams(collective_id=1, has_side_effects=True),
    )(r, w)


def transforms(freq_bin, slab_order):
    g = lax.axis_index("freq")
    slabs = lax.dynamic_slice_in_dim(slab_order, g * NTILE, NTILE)
    times = (slabs[:, None] * NT + jnp.arange(NT, dtype=jnp.int32)[None, :]).reshape(-1)
    total = NT * NTILE * NFREQ
    angles = (freq_bin[:, None] * times[None, :] % total).astype(F32) * (2.0 * math.pi / total)
    trig = jnp.stack([jnp.cos(angles), -jnp.sin(angles)], axis=1)
    eye = jnp.eye(NV, dtype=F32)
    fwd = (trig[:, :, None, :, None] * eye[None, None, :, None, :]).reshape(64, 256) / math.sqrt(total)
    inv = (trig.transpose(2, 0, 1)[:, None, :, :, None] * eye[None, :, None, None, :]).reshape(256, 64)
    inv = inv / math.sqrt(NFREQ)
    return jnp.concatenate(split(fwd), axis=0), jnp.concatenate(split(inv), axis=1)


def local(virtual_source_trace, v_bases, u_bases, ranks, freq_bin, slab_order):
    fwd, inv = transforms(freq_bin, slab_order)
    t = virtual_source_trace.reshape(NT, NV, COLS, EXT).transpose(3, 0, 1, 2).reshape(EXT, 16, COLS)
    t = jnp.pad(t, ((0, 0), (0, 0), (0, 128 - COLS)))
    x = spectra(t, fwd)
    v = v_bases[0].transpose(0, 2, 4, 3, 1)
    u = u_bases[0].transpose(0, 2, 4, 3, 1)
    r = apply(ranks.reshape(ROWS, 1, COLS), x, v, u)
    return output(r, inv).reshape(NT, NV, OUT)


def solution(mesh):
    in_specs = (
        P(("freq", "tile"), None, None),
        P("freq", "tile", None, None, None, None),
        P("freq", "tile", None, None, None, None),
        P("freq", "tile", None),
        P(),
        P(),
    )
    out_specs = P(("freq", "tile"), None, None)
    return jax.shard_map(local, mesh=mesh, in_specs=in_specs, out_specs=out_specs, check_vma=False)
```

```python
import functools
import math

import jax
import jax.numpy as jnp
from jax import lax
from jax.experimental import pallas as pl
from jax.experimental.pallas import tpu as pltpu
from jax.sharding import PartitionSpec as P

F32, BF16 = jnp.float32, jnp.bfloat16
MESH = pl.DeviceIdType.MESH
EXT = 70
COLS = 120
RANK = 32
NV = 4
NT = 4
ROWS = 12
NTILE = 16
NFREQ = 8
CHUNK = 5
OUT = 13440
NT_DIMS = (((1,), (1,)), ((), ()))


def chunk_start(k):
    return (k * (EXT - CHUNK) + 7) // (NTILE - 1)


def split(x):
    hi = x.astype(BF16)
    return hi, (x - hi.astype(F32)).astype(BF16)


def tree(xs):
    while len(xs) > 1:
        xs = [a + b for a, b in zip(xs[::2], xs[1::2])] + ([xs[-1]] if len(xs) % 2 else [])
    return xs[0]


def peers():
    g, k = lax.axis_index("freq"), lax.axis_index("tile")
    over_tile = [(d, lax.rem(k + d, NTILE)) for d in range(1, NTILE)]
    over_freq = [(d, lax.rem(g + d, NFREQ)) for d in range(1, NFREQ)]
    return g, k, over_tile, over_freq


def enter(over_tile, over_freq):
    barrier = pltpu.get_barrier_semaphore()
    for _, kk in over_tile:
        pl.semaphore_signal(barrier, inc=1, device_id={"tile": kk}, device_id_type=MESH)
    for _, f in over_freq:
        pl.semaphore_signal(barrier, inc=1, device_id={"freq": f}, device_id_type=MESH)
    pl.semaphore_wait(barrier, NTILE + NFREQ - 2)


def remote(src, dst, send, recv, axis, to):
    return pltpu.make_async_remote_copy(
        src_ref=src, dst_ref=dst, send_sem=send, recv_sem=recv, device_id={axis: to}, device_id_type=MESH
    )


def pick(index, ref, first, count):
    out = jnp.zeros(index.shape, jnp.int32)
    for n in range(count):
        out = jnp.where(index == n, ref[first + n], out)
    return out


def trig(freq, time, part):
    total = NT * NTILE * NFREQ
    turn = (freq * time + part * (total // 4)) & (total - 1)
    return jnp.cos(turn.astype(F32) * (2.0 * math.pi / total))


def iota(shape, axis):
    return lax.broadcasted_iota(jnp.int32, shape, axis)


def forward_matrix(freq_ref, slab_ref, g):
    row, col = iota((64, 1), 0), iota((1, 256), 1)
    freq = pick(row // 8, freq_ref, 0, NFREQ)
    time = pick(col // 16, slab_ref, g * NTILE, NTILE) * NT + (col // NV) % NT
    wave = trig(freq, time, (row // NV) % 2) * (1.0 / math.sqrt(NT * NTILE * NFREQ))
    hi, lo = split(jnp.where(row % NV == col % NV, wave, 0.0))
    return jnp.concatenate([hi, lo], axis=0)


def inverse_matrix(freq_ref, slab_ref, g):
    row, col = iota((256, 1), 0), iota((1, 128), 1)
    freq = pick((col % 64) // 8, freq_ref, 0, NFREQ)
    time = pick(row // 16, slab_ref, g * NTILE, NTILE) * NT + (row // NV) % NT
    wave = trig(freq, time, (col // NV) % 2) * (1.0 / math.sqrt(NFREQ))
    wave = jnp.where(row % NV == col % NV, wave, 0.0)
    hi = wave.astype(BF16).astype(F32)
    return jnp.where(col < 64, hi, wave - hi).astype(BF16)


def spectra_kernel(freq_ref, slab_ref, t_ref, x_ref, w_ref, a1, s2, b2, s3, b3, own, ss1, rs1, ss2, rs2, ss3, rs3):
    g, k, over_tile, over_freq = peers()
    enter(over_tile, over_freq)
    mine = pltpu.make_async_copy(t_ref.at[pl.ds(chunk_start(k), CHUNK)], a1.at[k], own)
    mine.start()
    sends = []
    for _, kk in over_tile:
        c = remote(t_ref.at[pl.ds(chunk_start(kk), CHUNK)], a1.at[k], ss1.at[kk], rs1.at[k], "tile", kk)
        c.start()
        sends.append(c)
    w_ref[...] = forward_matrix(freq_ref, slab_ref, g)
    mine.wait()
    for _, kk in over_tile:
        remote(t_ref.at[pl.ds(0, CHUNK)], a1.at[kk], ss1.at[kk], rs1.at[kk], "tile", kk).wait_recv()
    for p in range(CHUNK):
        data = a1[:, p].reshape(NTILE * 16, 128)
        both = jnp.dot(w_ref[...], data, preferred_element_type=F32)
        s2[:, p] = (both[:64] + both[64:]).reshape(NFREQ, 8, 128).astype(BF16)
    for _, f in over_freq:
        c = remote(s2.at[f], b2.at[g], ss2.at[f], rs2.at[g], "freq", f)
        c.start()
        sends.append(c)
    total = s2[g].astype(F32)
    for _, f in over_freq:
        remote(s2.at[f], b2.at[f], ss2.at[f], rs2.at[f], "freq", f).wait_recv()
        total = total + b2[f].astype(F32)
    s3[...] = total.astype(BF16)
    for _, kk in over_tile:
        c = remote(s3, b3.at[k], ss3.at[kk], rs3.at[k], "tile", kk)
        c.start()
        sends.append(c)
    b3[k] = s3[...]
    for _, kk in over_tile:
        remote(s3, b3.at[kk], ss3.at[kk], rs3.at[kk], "tile", kk).wait_recv()
    for kk in range(NTILE):
        for p in range(CHUNK):
            x = b3[kk, p].astype(F32)
            xr, xi = x[0:4], x[4:8]
            x_ref[chunk_start(kk) + p] = jnp.concatenate([xr, xi - xr, xr + xi, xr], axis=0)
    for c in sends:
        c.wait_send()


def spectra(freq_bin, slab_order, t):
    vmem = pl.BlockSpec(memory_space=pltpu.VMEM)
    smem = pl.BlockSpec(memory_space=pltpu.SMEM)
    dma = pltpu.SemaphoreType.DMA
    return pl.pallas_call(
        spectra_kernel,
        out_shape=jax.ShapeDtypeStruct((EXT, 16, 128), F32),
        in_specs=[smem, smem, vmem],
        out_specs=vmem,
        scratch_shapes=[
            pltpu.VMEM((128, 256), BF16),
            pltpu.VMEM((NTILE, CHUNK, 16, 128), BF16),
            pltpu.VMEM((NFREQ, CHUNK, 8, 128), BF16),
            pltpu.VMEM((NFREQ, CHUNK, 8, 128), BF16),
            pltpu.VMEM((CHUNK, 8, 128), BF16),
            pltpu.VMEM((NTILE, CHUNK, 8, 128), BF16),
            dma,
            dma((NTILE,)), dma((NTILE,)), dma((NFREQ,)), dma((NFREQ,)), dma((NTILE,)), dma((NTILE,)),
        ],
        compiler_params=pltpu.CompilerParams(collective_id=0, has_side_effects=True),
    )(freq_bin, slab_order, t)


def project(v_ref, x_ref, rank_row, ct):
    row = lax.broadcasted_iota(jnp.int32, (8, COLS), 0)
    for h in range(2):
        def body(p, acc):
            acc = list(acc)
            for a in range(2):
                r = 16 * h + 8 * a
                re = v_ref[0, 0, p, r:r + 8, :].astype(F32)
                im = v_ref[0, 1, p, r:r + 8, :].astype(F32)
                for n, b in enumerate((re + im, re, im)):
                    for v in range(NV):
                        m = 4 * n + v
                        acc[12 * a + m] += b * jnp.broadcast_to(x_ref[p, m:m + 1, :COLS], (8, COLS))
            return tuple(acc)

        acc = lax.fori_loop(0, EXT, body, (jnp.zeros((8, COLS), F32),) * 24, unroll=5)
        for a in range(2):
            keep = row + (16 * h + 8 * a) < rank_row
            for v in range(NV):
                k1, k2, k3 = (acc[12 * a + 4 * n + v] for n in range(3))
                re = jnp.where(keep, k1 - k3, 0.0).astype(BF16)
                im = jnp.where(keep, k1 + k2, 0.0).astype(BF16)
                n = 64 * a + 16 * v
                ct[h, n:n + 8, 0:COLS] = re
                ct[h, n:n + 8, 128:128 + COLS] = -im
                ct[h, n + 8:n + 16, 0:COLS] = im
                ct[h, n + 8:n + 16, 128:128 + COLS] = re


def expand(u_ref, ct, diag, step):
    low = lax.broadcasted_iota(jnp.int32, (step, 8, 128), 2) < 64
    for h in range(2):
        @pl.loop(0, EXT // step)
        def _(s):
            us = []
            for c in range(2):
                u = u_ref[0, c, pl.ds(s * step, step), 16 * h:16 * h + 16, :].reshape(step * 16, COLS)
                us.append(jnp.pad(u, ((0, 0), (0, 128 - COLS))))
            z = lax.dot_general(jnp.concatenate(us, axis=1), ct[h], NT_DIMS, preferred_element_type=F32)
            z = z.reshape(step, 2, 8, 128)
            diag[h, pl.ds(s * step * 8, step * 8), :] = jnp.where(low, z[:, 0], z[:, 1]).reshape(step * 8, 128)


def collect(diag):
    lane = lax.broadcasted_iota(jnp.int32, (EXT, 128), 1) % 8
    halves = []
    for h in range(2):
        tot = diag[h, pl.ds(0, EXT, stride=8), :]
        for b in range(1, 8):
            tot = jnp.where(lane == b, diag[h, pl.ds(b, EXT, stride=8), :], tot)
        halves.append(tot)
    hi, lo = split(jnp.concatenate(halves, axis=1))
    rows = lax.broadcasted_iota(jnp.int32, (8, 256), 0)
    lanes = lax.broadcasted_iota(jnp.int32, (8, 256), 1)
    pick = ((lanes % 64) // 8 == (rows % 4) * 2 + rows // 4).astype(BF16)
    dot = functools.partial(lax.dot_general, dimension_numbers=NT_DIMS, preferred_element_type=F32)
    return dot(pick, hi) + dot(pick, lo)


def apply_kernel(
    step, freq_ref, slab_ref, rank_ref, x_ref, v_ref, u_ref, out_ref,
    ct, diag, inv, s1, b1, s2, b2, ss1, rs1, ss2, rs2,
):
    i = pl.program_id(0)
    g, k, over_tile, over_freq = peers()
    barrier = pltpu.get_barrier_semaphore()

    @pl.when(i == 0)
    def _():
        for _, kk in over_tile:
            pl.semaphore_signal(barrier, inc=1, device_id={"tile": kk}, device_id_type=MESH)
        for _, f in over_freq:
            pl.semaphore_signal(barrier, inc=1, device_id={"freq": f}, device_id_type=MESH)
        ct[...] = jnp.zeros_like(ct)
        inv[...] = inverse_matrix(freq_ref, slab_ref, g)

    project(v_ref, x_ref, rank_ref[0], ct)
    expand(u_ref, ct, diag, step)
    piece = jnp.pad(collect(diag), ((0, 0), (0, 128 - EXT)))
    s1[i] = pltpu.roll(piece, lax.rem((k * ROWS + i) * EXT, 128), 1).astype(BF16)

    @pl.when(i == 0)
    def _():
        pl.semaphore_wait(barrier, NTILE + NFREQ - 2)

    for _, f in over_freq:
        remote(s1.at[i], b1.at[i, g], ss1.at[f], rs1.at[i, g], "freq", f).start()
    b1[i, g] = s1[i]

    def finish(n):
        for _, f in over_freq:
            remote(s1.at[n], b1.at[n, f], ss1.at[f], rs1.at[n, f], "freq", f).wait_recv()
        r = b1[n].reshape(64, 128)
        res = jnp.dot(inv[...], jnp.concatenate([r, r], axis=0), preferred_element_type=F32)
        s2[:, n] = res.reshape(NTILE, 16, 128).astype(BF16)
        for _, kk in over_tile:
            remote(s2.at[kk, n], b2.at[k, n], ss2.at[kk], rs2.at[k], "tile", kk).start()
        b2[k, n] = s2[k, n]

    @pl.when(i > 0)
    def _():
        finish(i - 1)

    @pl.when(i == ROWS - 1)
    def _():
        finish(i)
        for _, kk in over_tile:
            remote(s2.at[kk], b2.at[kk], ss2.at[kk], rs2.at[kk], "tile", kk).wait_recv()
        lane = iota((16, 128), 1)
        tiles = [[] for _ in range(OUT // 128)]
        for row in range(NTILE * ROWS):
            a, off = divmod(row * EXT, 128)
            val = b2[row // ROWS, row % ROWS]
            if off + EXT <= 128:
                tiles[a].append(val)
            else:
                tiles[a].append(jnp.where(lane >= off, val, jnp.zeros_like(val)))
                tiles[a + 1].append(jnp.where(lane < off, val, jnp.zeros_like(val)))
        for m, vals in enumerate(tiles):
            out_ref[:, 128 * m:128 * m + 128] = tree(vals)
        for _, f in over_freq:
            remote(s1, b1.at[:, f], ss1.at[f], rs1.at[0, f], "freq", f).wait_send()
        for _, kk in over_tile:
            remote(s2.at[kk], b2.at[kk], ss2.at[kk], rs2.at[kk], "tile", kk).wait_send()


def apply(freq_bin, slab_order, ranks, x, v, u, step=70):
    dma = pltpu.SemaphoreType.DMA
    smem = pl.BlockSpec(memory_space=pltpu.SMEM)
    bases = pl.BlockSpec((1, 2, EXT, RANK, COLS), lambda i: (i, 0, 0, 0, 0))
    return pl.pallas_call(
        functools.partial(apply_kernel, step),
        grid=(ROWS,),
        out_shape=jax.ShapeDtypeStruct((16, OUT), BF16),
        in_specs=[
            smem,
            smem,
            pl.BlockSpec((1, 1, COLS), lambda i: (i, 0, 0)),
            pl.BlockSpec((EXT, 16, 128), lambda i: (0, 0, 0)),
            bases,
            bases,
        ],
        out_specs=pl.BlockSpec((16, OUT), lambda i: (0, 0)),
        scratch_shapes=[
            pltpu.VMEM((2, 128, 256), BF16),
            pltpu.VMEM((2, EXT * 8, 128), F32),
            pltpu.VMEM((256, 128), BF16),
            pltpu.VMEM((ROWS, 8, 128), BF16),
            pltpu.VMEM((ROWS, NFREQ, 8, 128), BF16),
            pltpu.VMEM((NTILE, ROWS, 16, 128), BF16),
            pltpu.VMEM((NTILE, ROWS, 16, 128), BF16),
            dma((NFREQ,)), dma((ROWS, NFREQ)), dma((NTILE,)), dma((NTILE,)),
        ],
        compiler_params=pltpu.CompilerParams(collective_id=1, has_side_effects=True),
    )(freq_bin, slab_order, ranks, x, v, u)


def local(virtual_source_trace, v_bases, u_bases, ranks, freq_bin, slab_order):
    t = virtual_source_trace.reshape(NT, NV, COLS, EXT).transpose(3, 0, 1, 2).reshape(EXT, 16, COLS)
    t = jnp.pad(t, ((0, 0), (0, 0), (0, 128 - COLS)))
    x = spectra(freq_bin, slab_order, t)
    v = v_bases[0].transpose(0, 2, 4, 3, 1)
    u = u_bases[0].transpose(0, 2, 4, 3, 1)
    out = apply(freq_bin, slab_order, ranks.reshape(ROWS, 1, COLS), x, v, u)
    return out.reshape(NT, NV, OUT)


def solution(mesh):
    in_specs = (
        P(("freq", "tile"), None, None),
        P("freq", "tile", None, None, None, None),
        P("freq", "tile", None, None, None, None),
        P("freq", "tile", None),
        P(),
        P(),
    )
    out_specs = P(("freq", "tile"), None, None)
    return jax.shard_map(local, mesh=mesh, in_specs=in_specs, out_specs=out_specs, check_vma=False)
```

```python
import functools
import math

import jax
import jax.numpy as jnp
from jax import lax
from jax.experimental import pallas as pl
from jax.experimental.pallas import tpu as pltpu
from jax.sharding import PartitionSpec as P

F32, BF16 = jnp.float32, jnp.bfloat16
MESH = pl.DeviceIdType.MESH
EXT = 70
COLS = 120
RANK = 32
NV = 4
NT = 4
ROWS = 12
NTILE = 16
NFREQ = 8
CHUNK = 5
PARTS = ((0, 5),)
BATCH = 3
NB = ROWS // BATCH
OUT = 13440
NT_DIMS = (((1,), (1,)), ((), ()))


def chunk_start(k):
    return (k * (EXT - CHUNK) + 7) // (NTILE - 1)


def split(x):
    hi = x.astype(BF16)
    return hi, (x - hi.astype(F32)).astype(BF16)


def tree(xs):
    while len(xs) > 1:
        xs = [a + b for a, b in zip(xs[::2], xs[1::2])] + ([xs[-1]] if len(xs) % 2 else [])
    return xs[0]


def peers():
    g, k = lax.axis_index("freq"), lax.axis_index("tile")
    over_tile = [(d, lax.rem(k + d, NTILE)) for d in range(1, NTILE)]
    over_freq = [(d, lax.rem(g + d, NFREQ)) for d in range(1, NFREQ)]
    return g, k, over_tile, over_freq


def remote(src, dst, send, recv, axis, to):
    return pltpu.make_async_remote_copy(
        src_ref=src, dst_ref=dst, send_sem=send, recv_sem=recv, device_id={axis: to}, device_id_type=MESH
    )


def pick(index, ref, first, count):
    out = jnp.zeros(index.shape, jnp.int32)
    for n in range(count):
        out = jnp.where(index == n, ref[first + n], out)
    return out


def trig(freq, time, part):
    total = NT * NTILE * NFREQ
    turn = (freq * time + part * (total // 4)) & (total - 1)
    return jnp.cos(turn.astype(F32) * (2.0 * math.pi / total))


def iota(shape, axis):
    return lax.broadcasted_iota(jnp.int32, shape, axis)


def forward_matrix(freq_ref, slab_ref, g):
    row, col = iota((64, 1), 0), iota((1, 256), 1)
    freq = pick(row // 8, freq_ref, 0, NFREQ)
    time = pick(col // 16, slab_ref, g * NTILE, NTILE) * NT + (col // NV) % NT
    wave = trig(freq, time, (row // NV) % 2) * (1.0 / math.sqrt(NT * NTILE * NFREQ))
    hi, lo = split(jnp.where(row % NV == col % NV, wave, 0.0))
    return jnp.concatenate([hi, lo], axis=0)


def inverse_matrix(freq_ref, slab_ref, g):
    row, col = iota((256, 1), 0), iota((1, 128), 1)
    freq = pick((col % 64) // 8, freq_ref, 0, NFREQ)
    time = pick(row // 16, slab_ref, g * NTILE, NTILE) * NT + (row // NV) % NT
    wave = trig(freq, time, (col // NV) % 2) * (1.0 / math.sqrt(NFREQ))
    wave = jnp.where(row % NV == col % NV, wave, 0.0)
    hi = wave.astype(BF16).astype(F32)
    return jnp.where(col < 64, hi, wave - hi).astype(BF16)


def spectra(g, k, over_tile, over_freq, mats, t_ref, x_ref, w_ref, a1, s2, b2, s3, b3, own, ss1, rs1, ss2, rs2, ss3, rs3):
    mine = pltpu.make_async_copy(t_ref.at[pl.ds(chunk_start(k), CHUNK)], a1.at[k], own)
    mine.start()
    sends = []
    for n, (o, size) in enumerate(PARTS):
        for _, kk in over_tile:
            c = remote(
                t_ref.at[pl.ds(chunk_start(kk) + o, size)], a1.at[k, o:o + size], ss1.at[n, kk], rs1.at[n, k], "tile", kk
            )
            c.start()
            sends.append(c)
    mats()
    mine.wait()
    for n, (o, size) in enumerate(PARTS):
        for _, kk in over_tile:
            dst = a1.at[kk, o:o + size]
            remote(dst, dst, ss1.at[n, kk], rs1.at[n, kk], "tile", kk).wait_recv()
        for p in range(o, o + size):
            data = a1[:, p].reshape(NTILE * 16, COLS)
            both = jnp.dot(w_ref[...], data, preferred_element_type=F32)
            s2[:, p] = (both[:64] + both[64:]).reshape(NFREQ, 8, COLS).astype(BF16)
        for _, f in over_freq:
            c = remote(s2.at[f, o:o + size], b2.at[g, o:o + size], ss2.at[n, f], rs2.at[n, g], "freq", f)
            c.start()
            sends.append(c)
    for n, (o, size) in enumerate(PARTS):
        total = s2[g, o:o + size].astype(F32)
        for _, f in over_freq:
            dst = b2.at[f, o:o + size]
            remote(dst, dst, ss2.at[n, f], rs2.at[n, f], "freq", f).wait_recv()
            total = total + b2[f, o:o + size].astype(F32)
        s3[o:o + size] = total.astype(BF16)
        for _, kk in over_tile:
            c = remote(s3.at[o:o + size], b3.at[k, o:o + size], ss3.at[n, kk], rs3.at[n, k], "tile", kk)
            c.start()
            sends.append(c)
    b3[k] = s3[...]
    for n, (o, size) in enumerate(PARTS):
        for _, kk in over_tile:
            dst = b3.at[kk, o:o + size]
            remote(dst, dst, ss3.at[n, kk], rs3.at[n, kk], "tile", kk).wait_recv()
    for kk in range(NTILE):
        for p in range(CHUNK):
            x = b3[kk, p].astype(F32)
            xr, xi = x[0:4], x[4:8]
            x_ref[chunk_start(kk) + p] = jnp.concatenate([xr, xi - xr, xr + xi, xr], axis=0)
    for c in sends:
        c.wait_send()


def project(v_ref, x_ref, rank_row, ct):
    row = lax.broadcasted_iota(jnp.int32, (8, COLS), 0)
    for h in range(2):
        def body(p, acc):
            acc = list(acc)
            for a in range(2):
                r = 16 * h + 8 * a
                re = v_ref[0, p, r:r + 8, :].astype(F32)
                im = v_ref[1, p, r:r + 8, :].astype(F32)
                for n, b in enumerate((re + im, re, im)):
                    for v in range(NV):
                        m = 4 * n + v
                        acc[12 * a + m] += b * jnp.broadcast_to(x_ref[p, m:m + 1, :COLS], (8, COLS))
            return tuple(acc)

        acc = lax.fori_loop(0, EXT, body, (jnp.zeros((8, COLS), F32),) * 24, unroll=5)
        for a in range(2):
            keep = row + (16 * h + 8 * a) < rank_row
            for v in range(NV):
                k1, k2, k3 = (acc[12 * a + 4 * n + v] for n in range(3))
                re = jnp.where(keep, k1 - k3, 0.0).astype(BF16)
                im = jnp.where(keep, k1 + k2, 0.0).astype(BF16)
                n = 128 * h + 64 * a + 16 * v
                ct[n:n + 8, 0:COLS] = re
                ct[n:n + 8, 128:128 + COLS] = -im
                ct[n + 8:n + 16, 0:COLS] = im
                ct[n + 8:n + 16, 128:128 + COLS] = re


def expand(u_ref, ct, diag):
    low = iota((EXT, 8, 128), 2) < 64
    us = [jnp.pad(u_ref[c].reshape(EXT * RANK, COLS), ((0, 0), (0, 128 - COLS))) for c in range(2)]
    z = lax.dot_general(jnp.concatenate(us, axis=1), ct[...], NT_DIMS, preferred_element_type=F32)
    z = z.reshape(EXT, 4, 8, 256)
    for h in range(2):
        lanes = slice(128 * h, 128 * h + 128)
        diag[h] = jnp.where(low, z[:, 2 * h, :, lanes], z[:, 2 * h + 1, :, lanes]).reshape(EXT * 8, 128)


def collect(diag):
    lane = lax.broadcasted_iota(jnp.int32, (EXT, 128), 1) % 8
    halves = []
    for h in range(2):
        tot = diag[h, pl.ds(0, EXT, stride=8), :]
        for b in range(1, 8):
            tot = jnp.where(lane == b, diag[h, pl.ds(b, EXT, stride=8), :], tot)
        halves.append(tot)
    hi, lo = split(jnp.concatenate(halves, axis=1))
    rows = lax.broadcasted_iota(jnp.int32, (8, 256), 0)
    lanes = lax.broadcasted_iota(jnp.int32, (8, 256), 1)
    pick = ((lanes % 64) // 8 == (rows % 4) * 2 + rows // 4).astype(BF16)
    dot = functools.partial(lax.dot_general, dimension_numbers=NT_DIMS, preferred_element_type=F32)
    return dot(pick, hi) + dot(pick, lo)


def apply_kernel(
    freq_ref, slab_ref, t_ref, rank_ref, v_hbm, u_hbm, b2,
    v_all, u_all, x_ref, w_ref, ct, diag, inv, ring, s1, b1, s2, vs, us, ss1, rs1, ss2, rs2, own, *scratch
):
    i = pl.program_id(0)
    g, k, over_tile, over_freq = peers()
    barrier = pltpu.get_barrier_semaphore()

    @pl.when(i == 0)
    def _():
        for _, kk in over_tile:
            pl.semaphore_signal(barrier, inc=1, device_id={"tile": kk}, device_id_type=MESH)
        for _, f in over_freq:
            pl.semaphore_signal(barrier, inc=1, device_id={"freq": f}, device_id_type=MESH)
        for n in range(ROWS):
            pltpu.make_async_copy(v_hbm.at[n], v_all.at[n], vs.at[n]).start()
            pltpu.make_async_copy(u_hbm.at[n], u_all.at[n], us.at[n]).start()
        ct[...] = jnp.zeros_like(ct)

        def mats():
            w_ref[...] = forward_matrix(freq_ref, slab_ref, g)
            inv[...] = inverse_matrix(freq_ref, slab_ref, g)

        pl.semaphore_wait(barrier, NTILE + NFREQ - 2)
        spectra(g, k, over_tile, over_freq, mats, t_ref, x_ref, w_ref, *scratch)

    pltpu.make_async_copy(v_hbm.at[i], v_all.at[i], vs.at[i]).wait()
    project(v_all.at[i], x_ref, rank_ref[i], ct)
    pltpu.make_async_copy(u_hbm.at[i], u_all.at[i], us.at[i]).wait()
    expand(u_all.at[i], ct, diag)
    piece = jnp.pad(collect(diag), ((0, 0), (0, 128 - EXT)))
    batch, turn = lax.div(i, BATCH), lax.rem(i, BATCH)
    start = (k * ROWS + i) * EXT
    off = lax.rem(start, 128)
    piece = pltpu.roll(piece, off, 1)
    head = iota((8, 128), 1) >= off
    odd = lax.rem(lax.div(start, 128), 2) == 1
    for t in range(2):
        before = jnp.where(turn == 0, 0.0, ring[t])
        ring[t] = before + jnp.where(head == (odd if t else jnp.logical_not(odd)), piece, 0.0)

    def finish(n):
        for _, f in over_freq:
            remote(s1.at[n], b1.at[n, f], ss1.at[f], rs1.at[n, f], "freq", f).wait_recv()
        r = b1[n].reshape(64, 256)
        res = jnp.dot(inv[...], jnp.concatenate([r, r], axis=0), preferred_element_type=F32)
        s2[:, n] = res.reshape(NTILE, 16, 256).astype(BF16)
        for _, kk in over_tile:
            remote(s2.at[kk, n], b2.at[k, n], ss2.at[kk], rs2.at[k], "tile", kk).start()
        pltpu.make_async_copy(s2.at[k, n], b2.at[k, n], own.at[n]).start()

    @pl.when(jnp.logical_and(turn == 0, i > 0))
    def _():
        finish(batch - 1)

    @pl.when(turn == BATCH - 1)
    def _():
        s1[batch] = jnp.concatenate([ring[0], ring[1]], axis=1).astype(BF16)
        for _, f in over_freq:
            remote(s1.at[batch], b1.at[batch, g], ss1.at[f], rs1.at[batch, g], "freq", f).start()
        b1[batch, g] = s1[batch]

    @pl.when(i == ROWS - 1)
    def _():
        finish(NB - 1)
        for _, kk in over_tile:
            remote(s2.at[kk], b2.at[kk], ss2.at[kk], rs2.at[kk], "tile", kk).wait_recv()
        for n in range(NB):
            pltpu.make_async_copy(s2.at[k, n], b2.at[k, n], own.at[n]).wait()
        for _, f in over_freq:
            remote(s1, b1.at[:, f], ss1.at[f], rs1.at[0, f], "freq", f).wait_send()
        for _, kk in over_tile:
            remote(s2.at[kk], b2.at[kk], ss2.at[kk], rs2.at[kk], "tile", kk).wait_send()


def apply(freq_bin, slab_order, t, ranks, v, u):
    dma = pltpu.SemaphoreType.DMA
    smem = pl.BlockSpec(memory_space=pltpu.SMEM)
    vmem = pl.BlockSpec(memory_space=pltpu.VMEM)
    hbm = pl.BlockSpec(memory_space=pl.ANY)
    return pl.pallas_call(
        apply_kernel,
        grid=(ROWS,),
        out_shape=jax.ShapeDtypeStruct((NTILE, NB, 16, 256), BF16),
        in_specs=[smem, smem, vmem, vmem, hbm, hbm],
        out_specs=hbm,
        scratch_shapes=[
            pltpu.VMEM((ROWS, 2, EXT, RANK, COLS), BF16),
            pltpu.VMEM((ROWS, 2, EXT, RANK, COLS), BF16),
            pltpu.VMEM((EXT, 16, COLS), F32),
            pltpu.VMEM((128, 256), BF16),
            pltpu.VMEM((256, 256), BF16),
            pltpu.VMEM((2, EXT * 8, 128), F32),
            pltpu.VMEM((256, 128), BF16),
            pltpu.VMEM((2, 8, 128), F32),
            pltpu.VMEM((NB, 8, 256), BF16),
            pltpu.VMEM((NB, NFREQ, 8, 256), BF16),
            pltpu.VMEM((NTILE, NB, 16, 256), BF16),
            dma((ROWS,)), dma((ROWS,)),
            dma((NFREQ,)), dma((NB, NFREQ)), dma((NTILE,)), dma((NTILE,)), dma((NB,)),
            pltpu.VMEM((NTILE, CHUNK, 16, COLS), BF16),
            pltpu.VMEM((NFREQ, CHUNK, 8, COLS), BF16),
            pltpu.VMEM((NFREQ, CHUNK, 8, COLS), BF16),
            pltpu.VMEM((CHUNK, 8, COLS), BF16),
            pltpu.VMEM((NTILE, CHUNK, 8, COLS), BF16),
            dma,
            *(dma((len(PARTS), n)) for n in (NTILE, NTILE, NFREQ, NFREQ, NTILE, NTILE)),
        ],
        compiler_params=pltpu.CompilerParams(collective_id=0, has_side_effects=True),
    )(freq_bin, slab_order, t, ranks, v, u)


def assemble_kernel(b_ref, out_ref):
    lane = iota((16, 128), 1)
    width = BATCH * EXT
    for m in range(OUT // 128):
        vals = []
        for row in range(128 * m // width, (128 * m + 127) // width + 1):
            val = b_ref[row // NB, row % NB, :, 128 * (m % 2):128 * (m % 2) + 128]
            lo, hi = row * width - 128 * m, (row + 1) * width - 128 * m
            if lo > 0:
                val = jnp.where(lane >= lo, val, jnp.zeros_like(val))
            if hi < 128:
                val = jnp.where(lane < hi, val, jnp.zeros_like(val))
            vals.append(val)
        val = tree(vals)
        for t in range(NT):
            out_ref[t, m] = val[NV * t:NV * t + NV]


def assemble(b):
    vmem = pl.BlockSpec(memory_space=pltpu.VMEM)
    return pl.pallas_call(
        assemble_kernel,
        out_shape=jax.ShapeDtypeStruct((NT, OUT // 128, NV, 128), BF16),
        in_specs=[vmem],
        out_specs=vmem,
    )(b)


def local(virtual_source_trace, v_bases, u_bases, ranks, freq_bin, slab_order):
    t = virtual_source_trace.reshape(NT, NV, COLS, EXT).transpose(3, 0, 1, 2).reshape(EXT, 16, COLS)
    v = v_bases[0].transpose(0, 2, 4, 3, 1)
    u = u_bases[0].transpose(0, 2, 4, 3, 1)
    out = assemble(apply(freq_bin, slab_order, t, ranks.reshape(ROWS, 1, COLS), v, u))
    return out.transpose(0, 2, 1, 3).reshape(NT, NV, OUT)


def solution(mesh):
    in_specs = (
        P(("freq", "tile"), None, None),
        P("freq", "tile", None, None, None, None),
        P("freq", "tile", None, None, None, None),
        P("freq", "tile", None),
        P(),
        P(),
    )
    out_specs = P(("freq", "tile"), None, None)
    return jax.shard_map(local, mesh=mesh, in_specs=in_specs, out_specs=out_specs, check_vma=False)
```

```python
import functools
import math

import jax
import jax.numpy as jnp
from jax import lax
from jax.experimental import pallas as pl
from jax.experimental.pallas import tpu as pltpu
from jax.sharding import PartitionSpec as P

F32, BF16 = jnp.float32, jnp.bfloat16
MESH = pl.DeviceIdType.MESH
EXT = 70
COLS = 120
RANK = 32
NV = 4
NT = 4
ROWS = 12
NTILE = 16
NFREQ = 8
CHUNK = 5
PARTS = ((0, 5),)
BATCH = 3
NB = ROWS // BATCH
OUT = 13440
NT_DIMS = (((1,), (1,)), ((), ()))


def chunk_start(k):
    return (k * (EXT - CHUNK) + 7) // (NTILE - 1)


def split(x):
    hi = x.astype(BF16)
    return hi, (x - hi.astype(F32)).astype(BF16)


def tree(xs):
    while len(xs) > 1:
        xs = [a + b for a, b in zip(xs[::2], xs[1::2])] + ([xs[-1]] if len(xs) % 2 else [])
    return xs[0]


def peers():
    g, k = lax.axis_index("freq"), lax.axis_index("tile")
    over_tile = [(d, lax.rem(k + d, NTILE)) for d in range(1, NTILE)]
    over_freq = [(d, lax.rem(g + d, NFREQ)) for d in range(1, NFREQ)]
    return g, k, over_tile, over_freq


def remote(src, dst, send, recv, axis, to):
    return pltpu.make_async_remote_copy(
        src_ref=src, dst_ref=dst, send_sem=send, recv_sem=recv, device_id={axis: to}, device_id_type=MESH
    )


def pick(index, ref, first, count):
    out = jnp.zeros(index.shape, jnp.int32)
    for n in range(count):
        out = jnp.where(index == n, ref[first + n], out)
    return out


def trig(freq, time, part):
    total = NT * NTILE * NFREQ
    turn = (freq * time + part * (total // 4)) & (total - 1)
    return jnp.cos(turn.astype(F32) * (2.0 * math.pi / total))


def iota(shape, axis):
    return lax.broadcasted_iota(jnp.int32, shape, axis)


def forward_matrix(freq_ref, slab_ref, g):
    row, col = iota((64, 1), 0), iota((1, 256), 1)
    freq = pick(row // 8, freq_ref, 0, NFREQ)
    time = pick(col // 16, slab_ref, g * NTILE, NTILE) * NT + (col // NV) % NT
    wave = trig(freq, time, (row // NV) % 2) * (1.0 / math.sqrt(NT * NTILE * NFREQ))
    hi, lo = split(jnp.where(row % NV == col % NV, wave, 0.0))
    return jnp.concatenate([hi, lo], axis=0)


def inverse_matrix(freq_ref, slab_ref, g):
    row, col = iota((256, 1), 0), iota((1, 128), 1)
    freq = pick((col % 64) // 8, freq_ref, 0, NFREQ)
    time = pick(row // 16, slab_ref, g * NTILE, NTILE) * NT + (row // NV) % NT
    wave = trig(freq, time, (col // NV) % 2) * (1.0 / math.sqrt(NFREQ))
    wave = jnp.where(row % NV == col % NV, wave, 0.0)
    hi = wave.astype(BF16).astype(F32)
    return jnp.where(col < 64, hi, wave - hi).astype(BF16)


def spectra(g, k, over_tile, over_freq, mats, t_ref, x_ref, w_ref, a1, s2, b2, s3, b3, own, ss1, rs1, ss2, rs2, ss3, rs3):
    mine = pltpu.make_async_copy(t_ref.at[pl.ds(chunk_start(k), CHUNK)], a1.at[k], own)
    mine.start()
    sends = []
    for n, (o, size) in enumerate(PARTS):
        for _, kk in over_tile:
            c = remote(
                t_ref.at[pl.ds(chunk_start(kk) + o, size)], a1.at[k, o:o + size], ss1.at[n, kk], rs1.at[n, k], "tile", kk
            )
            c.start()
            sends.append(c)
    mats()
    mine.wait()
    for n, (o, size) in enumerate(PARTS):
        for _, kk in over_tile:
            dst = a1.at[kk, o:o + size]
            remote(dst, dst, ss1.at[n, kk], rs1.at[n, kk], "tile", kk).wait_recv()
        for p in range(o, o + size):
            data = a1[:, p].reshape(NTILE * 16, COLS)
            both = jnp.dot(w_ref[...], data, preferred_element_type=F32)
            s2[:, p] = (both[:64] + both[64:]).reshape(NFREQ, 8, COLS).astype(BF16)
        for _, f in over_freq:
            c = remote(s2.at[f, o:o + size], b2.at[g, o:o + size], ss2.at[n, f], rs2.at[n, g], "freq", f)
            c.start()
            sends.append(c)
    for n, (o, size) in enumerate(PARTS):
        total = s2[g, o:o + size].astype(F32)
        for _, f in over_freq:
            dst = b2.at[f, o:o + size]
            remote(dst, dst, ss2.at[n, f], rs2.at[n, f], "freq", f).wait_recv()
            total = total + b2[f, o:o + size].astype(F32)
        s3[o:o + size] = total.astype(BF16)
        for _, kk in over_tile:
            c = remote(s3.at[o:o + size], b3.at[k, o:o + size], ss3.at[n, kk], rs3.at[n, k], "tile", kk)
            c.start()
            sends.append(c)
    b3[k] = s3[...]
    for n, (o, size) in enumerate(PARTS):
        for _, kk in over_tile:
            dst = b3.at[kk, o:o + size]
            remote(dst, dst, ss3.at[n, kk], rs3.at[n, kk], "tile", kk).wait_recv()
    for kk in range(NTILE):
        for p in range(CHUNK):
            x = b3[kk, p].astype(F32)
            xr, xi = x[0:4], x[4:8]
            x_ref[chunk_start(kk) + p] = jnp.concatenate([xr, xi - xr, xr + xi, xr], axis=0)
    for c in sends:
        c.wait_send()


def project(v_ref, x_ref, rank_row, ct):
    row = lax.broadcasted_iota(jnp.int32, (8, COLS), 0)
    for h in range(2):
        def body(p, acc):
            acc = list(acc)
            for a in range(2):
                r = 16 * h + 8 * a
                re = v_ref[0, p, r:r + 8, :].astype(F32)
                im = v_ref[1, p, r:r + 8, :].astype(F32)
                for n, b in enumerate((re + im, re, im)):
                    for v in range(NV):
                        m = 4 * n + v
                        acc[12 * a + m] += b * jnp.broadcast_to(x_ref[p, m:m + 1, :COLS], (8, COLS))
            return tuple(acc)

        acc = lax.fori_loop(0, EXT, body, (jnp.zeros((8, COLS), F32),) * 24, unroll=35)
        for a in range(2):
            keep = row + (16 * h + 8 * a) < rank_row
            for v in range(NV):
                k1, k2, k3 = (acc[12 * a + 4 * n + v] for n in range(3))
                re = jnp.where(keep, k1 - k3, 0.0).astype(BF16)
                im = jnp.where(keep, k1 + k2, 0.0).astype(BF16)
                n = 128 * h + 64 * a + 16 * v
                ct[n:n + 8, 0:COLS] = re
                ct[n:n + 8, 128:128 + COLS] = -im
                ct[n + 8:n + 16, 0:COLS] = im
                ct[n + 8:n + 16, 128:128 + COLS] = re


def expand(u_ref, ct, diag):
    low = iota((EXT, 8, 128), 2) < 64
    us = [jnp.pad(u_ref[c].reshape(EXT * RANK, COLS), ((0, 0), (0, 128 - COLS))) for c in range(2)]
    z = lax.dot_general(jnp.concatenate(us, axis=1), ct[...], NT_DIMS, preferred_element_type=F32)
    z = z.reshape(EXT, 4, 8, 256)
    for h in range(2):
        lanes = slice(128 * h, 128 * h + 128)
        diag[h] = jnp.where(low, z[:, 2 * h, :, lanes], z[:, 2 * h + 1, :, lanes]).reshape(EXT * 8, 128)


def collect(diag):
    lane = lax.broadcasted_iota(jnp.int32, (EXT, 128), 1) % 8
    halves = []
    for h in range(2):
        tot = diag[h, pl.ds(0, EXT, stride=8), :]
        for b in range(1, 8):
            tot = jnp.where(lane == b, diag[h, pl.ds(b, EXT, stride=8), :], tot)
        halves.append(tot)
    hi, lo = split(jnp.concatenate(halves, axis=1))
    rows = lax.broadcasted_iota(jnp.int32, (8, 256), 0)
    lanes = lax.broadcasted_iota(jnp.int32, (8, 256), 1)
    pick = ((lanes % 64) // 8 == (rows % 4) * 2 + rows // 4).astype(BF16)
    dot = functools.partial(lax.dot_general, dimension_numbers=NT_DIMS, preferred_element_type=F32)
    return dot(pick, hi) + dot(pick, lo)


def apply_kernel(
    freq_ref, slab_ref, t_ref, rank_ref, v_hbm, u_hbm, b2,
    v_all, u_all, x_ref, w_ref, ct, diag, inv, ring, s1, b1, s2, vs, us, ss1, rs1, ss2, rs2, own, *scratch
):
    i = pl.program_id(0)
    g, k, over_tile, over_freq = peers()
    barrier = pltpu.get_barrier_semaphore()

    @pl.when(i == 0)
    def _():
        for _, kk in over_tile:
            pl.semaphore_signal(barrier, inc=1, device_id={"tile": kk}, device_id_type=MESH)
        for _, f in over_freq:
            pl.semaphore_signal(barrier, inc=1, device_id={"freq": f}, device_id_type=MESH)
        for n in range(ROWS):
            pltpu.make_async_copy(v_hbm.at[n], v_all.at[n], vs.at[n]).start()
            pltpu.make_async_copy(u_hbm.at[n], u_all.at[n], us.at[n]).start()
        ct[...] = jnp.zeros_like(ct)
        diag[...] = jnp.zeros_like(diag)

        def mats():
            w_ref[...] = forward_matrix(freq_ref, slab_ref, g)
            inv[...] = inverse_matrix(freq_ref, slab_ref, g)

        pl.semaphore_wait(barrier, NTILE + NFREQ - 2)
        spectra(g, k, over_tile, over_freq, mats, t_ref, x_ref, w_ref, *scratch)

    pltpu.make_async_copy(v_hbm.at[i], v_all.at[i], vs.at[i]).wait()
    project(v_all.at[i], x_ref, rank_ref[i], ct)
    pltpu.make_async_copy(u_hbm.at[i], u_all.at[i], us.at[i]).wait()

    def place(n, piece):
        start = (k * ROWS + n) * EXT
        off = lax.rem(start, 128)
        piece = pltpu.roll(jnp.pad(piece, ((0, 0), (0, 128 - EXT))), off, 1)
        head = iota((8, 128), 1) >= off
        odd = lax.rem(lax.div(start, 128), 2) == 1
        for t in range(2):
            before = jnp.where(lax.rem(n, BATCH) == 0, 0.0, ring[t])
            ring[t] = before + jnp.where(head == (odd if t else jnp.logical_not(odd)), piece, 0.0)

    def send(n):
        s1[n] = jnp.concatenate([ring[0], ring[1]], axis=1).astype(BF16)
        for _, f in over_freq:
            remote(s1.at[n], b1.at[n, g], ss1.at[f], rs1.at[n, g], "freq", f).start()
        b1[n, g] = s1[n]

    def finish(n):
        for _, f in over_freq:
            remote(s1.at[n], b1.at[n, f], ss1.at[f], rs1.at[n, f], "freq", f).wait_recv()
        r = b1[n].reshape(64, 256)
        res = jnp.dot(inv[...], jnp.concatenate([r, r], axis=0), preferred_element_type=F32)
        s2[:, n] = res.reshape(NTILE, 16, 256).astype(BF16)
        for _, kk in over_tile:
            remote(s2.at[kk, n], b2.at[k, n], ss2.at[kk], rs2.at[k], "tile", kk).start()
        pltpu.make_async_copy(s2.at[k, n], b2.at[k, n], own.at[n]).start()

    last = collect(diag)
    expand(u_all.at[i], ct, diag)
    place(jnp.maximum(i - 1, 0), last)

    @pl.when(jnp.logical_and(lax.rem(i, BATCH) == 0, i > 0))
    def _():
        send(lax.div(i, BATCH) - 1)

    @pl.when(jnp.logical_and(lax.rem(i, BATCH) == 1, i > BATCH))
    def _():
        finish(lax.div(i, BATCH) - 1)

    @pl.when(i == ROWS - 1)
    def _():
        place(i, collect(diag))
        send(NB - 1)
        finish(NB - 1)
        for _, kk in over_tile:
            remote(s2.at[kk], b2.at[kk], ss2.at[kk], rs2.at[kk], "tile", kk).wait_recv()
        for n in range(NB):
            pltpu.make_async_copy(s2.at[k, n], b2.at[k, n], own.at[n]).wait()
        for _, f in over_freq:
            remote(s1, b1.at[:, f], ss1.at[f], rs1.at[0, f], "freq", f).wait_send()
        for _, kk in over_tile:
            remote(s2.at[kk], b2.at[kk], ss2.at[kk], rs2.at[kk], "tile", kk).wait_send()


def apply(freq_bin, slab_order, t, ranks, v, u):
    dma = pltpu.SemaphoreType.DMA
    smem = pl.BlockSpec(memory_space=pltpu.SMEM)
    vmem = pl.BlockSpec(memory_space=pltpu.VMEM)
    hbm = pl.BlockSpec(memory_space=pl.ANY)
    return pl.pallas_call(
        apply_kernel,
        grid=(ROWS,),
        out_shape=jax.ShapeDtypeStruct((NTILE, NB, 16, 256), BF16),
        in_specs=[smem, smem, vmem, vmem, hbm, hbm],
        out_specs=hbm,
        scratch_shapes=[
            pltpu.VMEM((ROWS, 2, EXT, RANK, COLS), BF16),
            pltpu.VMEM((ROWS, 2, EXT, RANK, COLS), BF16),
            pltpu.VMEM((EXT, 16, COLS), F32),
            pltpu.VMEM((128, 256), BF16),
            pltpu.VMEM((256, 256), BF16),
            pltpu.VMEM((2, EXT * 8, 128), F32),
            pltpu.VMEM((256, 128), BF16),
            pltpu.VMEM((2, 8, 128), F32),
            pltpu.VMEM((NB, 8, 256), BF16),
            pltpu.VMEM((NB, NFREQ, 8, 256), BF16),
            pltpu.VMEM((NTILE, NB, 16, 256), BF16),
            dma((ROWS,)), dma((ROWS,)),
            dma((NFREQ,)), dma((NB, NFREQ)), dma((NTILE,)), dma((NTILE,)), dma((NB,)),
            pltpu.VMEM((NTILE, CHUNK, 16, COLS), BF16),
            pltpu.VMEM((NFREQ, CHUNK, 8, COLS), BF16),
            pltpu.VMEM((NFREQ, CHUNK, 8, COLS), BF16),
            pltpu.VMEM((CHUNK, 8, COLS), BF16),
            pltpu.VMEM((NTILE, CHUNK, 8, COLS), BF16),
            dma,
            *(dma((len(PARTS), n)) for n in (NTILE, NTILE, NFREQ, NFREQ, NTILE, NTILE)),
        ],
        compiler_params=pltpu.CompilerParams(collective_id=0, has_side_effects=True),
    )(freq_bin, slab_order, t, ranks, v, u)


def assemble_kernel(b_ref, out_ref):
    lane = iota((16, 128), 1)
    width = BATCH * EXT
    for m in range(OUT // 128):
        vals = []
        for row in range(128 * m // width, (128 * m + 127) // width + 1):
            val = b_ref[row // NB, row % NB, :, 128 * (m % 2):128 * (m % 2) + 128]
            lo, hi = row * width - 128 * m, (row + 1) * width - 128 * m
            if lo > 0:
                val = jnp.where(lane >= lo, val, jnp.zeros_like(val))
            if hi < 128:
                val = jnp.where(lane < hi, val, jnp.zeros_like(val))
            vals.append(val)
        val = tree(vals)
        for t in range(NT):
            out_ref[t, m] = val[NV * t:NV * t + NV]


def assemble(b):
    vmem = pl.BlockSpec(memory_space=pltpu.VMEM)
    return pl.pallas_call(
        assemble_kernel,
        out_shape=jax.ShapeDtypeStruct((NT, OUT // 128, NV, 128), BF16),
        in_specs=[vmem],
        out_specs=vmem,
    )(b)


def local(virtual_source_trace, v_bases, u_bases, ranks, freq_bin, slab_order):
    t = virtual_source_trace.reshape(NT, NV, COLS, EXT).transpose(3, 0, 1, 2).reshape(EXT, 16, COLS)
    v = v_bases[0].transpose(0, 2, 4, 3, 1)
    u = u_bases[0].transpose(0, 2, 4, 3, 1)
    out = assemble(apply(freq_bin, slab_order, t, ranks.reshape(ROWS, 1, COLS), v, u))
    return out.transpose(0, 2, 1, 3).reshape(NT, NV, OUT)


def solution(mesh):
    in_specs = (
        P(("freq", "tile"), None, None),
        P("freq", "tile", None, None, None, None),
        P("freq", "tile", None, None, None, None),
        P("freq", "tile", None),
        P(),
        P(),
    )
    out_specs = P(("freq", "tile"), None, None)
    return jax.shard_map(local, mesh=mesh, in_specs=in_specs, out_specs=out_specs, check_vma=False)
```

```python
import functools
import math

import jax
import jax.numpy as jnp
from jax import lax
from jax.experimental import pallas as pl
from jax.experimental.pallas import tpu as pltpu
from jax.sharding import PartitionSpec as P

F32, BF16 = jnp.float32, jnp.bfloat16
MESH = pl.DeviceIdType.MESH
EXT = 70
COLS = 120
RANK = 32
NV = 4
NT = 4
ROWS = 12
NTILE = 16
NFREQ = 8
CHUNK = 5
PARTS = ((0, 5),)
BATCH = 3
NB = ROWS // BATCH
OUT = 13440
NT_DIMS = (((1,), (1,)), ((), ()))


def chunk_start(k):
    return (k * (EXT - CHUNK) + 7) // (NTILE - 1)


def split(x):
    hi = x.astype(BF16)
    return hi, (x - hi.astype(F32)).astype(BF16)


def tree(xs):
    while len(xs) > 1:
        xs = [a + b for a, b in zip(xs[::2], xs[1::2])] + ([xs[-1]] if len(xs) % 2 else [])
    return xs[0]


def peers():
    g, k = lax.axis_index("freq"), lax.axis_index("tile")
    far = (0, 1, 2, 1)
    steps = sorted(range(1, NTILE), key=lambda d: -far[d // 4] - far[d % 4])
    over_tile = [(d, lax.rem(k // 4 + d // 4, 4) * 4 + lax.rem(k % 4 + d % 4, 4)) for d in steps]
    steps = sorted(range(1, NFREQ), key=lambda d: -far[d // 2])
    over_freq = [(d, lax.rem(g // 2 + d // 2, 4) * 2 + lax.rem(g % 2 + d % 2, 2)) for d in steps]
    return g, k, over_tile, over_freq


def remote(src, dst, send, recv, axis, to):
    return pltpu.make_async_remote_copy(
        src_ref=src, dst_ref=dst, send_sem=send, recv_sem=recv, device_id={axis: to}, device_id_type=MESH
    )


def pick(index, ref, first, count):
    out = jnp.zeros(index.shape, jnp.int32)
    for n in range(count):
        out = jnp.where(index == n, ref[first + n], out)
    return out


def trig(freq, time, part):
    total = NT * NTILE * NFREQ
    turn = (freq * time + part * (total // 4)) & (total - 1)
    return jnp.cos(turn.astype(F32) * (2.0 * math.pi / total))


def iota(shape, axis):
    return lax.broadcasted_iota(jnp.int32, shape, axis)


def forward_matrix(freq_ref, slab_ref, g):
    row, col = iota((64, 1), 0), iota((1, 256), 1)
    freq = pick(row // 8, freq_ref, 0, NFREQ)
    time = pick(col // 16, slab_ref, g * NTILE, NTILE) * NT + (col // NV) % NT
    wave = trig(freq, time, (row // NV) % 2) * (1.0 / math.sqrt(NT * NTILE * NFREQ))
    hi, lo = split(jnp.where(row % NV == col % NV, wave, 0.0))
    return jnp.concatenate([hi, lo], axis=0)


def inverse_matrix(freq_ref, slab_ref, g):
    row, col = iota((256, 1), 0), iota((1, 128), 1)
    freq = pick((col % 64) // 8, freq_ref, 0, NFREQ)
    time = pick(row // 16, slab_ref, g * NTILE, NTILE) * NT + (row // NV) % NT
    wave = trig(freq, time, (col // NV) % 2) * (1.0 / math.sqrt(NFREQ))
    wave = jnp.where(row % NV == col % NV, wave, 0.0)
    hi = wave.astype(BF16).astype(F32)
    return jnp.where(col < 64, hi, wave - hi).astype(BF16)


def spectra(g, k, over_tile, over_freq, mats, t_ref, x_ref, w_ref, a1, s2, b2, s3, b3, own, ss1, rs1, ss2, rs2, ss3, rs3):
    mine = pltpu.make_async_copy(t_ref.at[pl.ds(chunk_start(k), CHUNK)], a1.at[k], own)
    mine.start()
    sends = []
    for n, (o, size) in enumerate(PARTS):
        for _, kk in over_tile:
            c = remote(
                t_ref.at[pl.ds(chunk_start(kk) + o, size)], a1.at[k, o:o + size], ss1.at[n, kk], rs1.at[n, k], "tile", kk
            )
            c.start()
            sends.append(c)
    mats()
    mine.wait()
    for n, (o, size) in enumerate(PARTS):
        for _, kk in over_tile:
            dst = a1.at[kk, o:o + size]
            remote(dst, dst, ss1.at[n, kk], rs1.at[n, kk], "tile", kk).wait_recv()
        for p in range(o, o + size):
            data = a1[:, p].reshape(NTILE * 16, COLS)
            both = jnp.dot(w_ref[...], data, preferred_element_type=F32)
            s2[:, p] = (both[:64] + both[64:]).reshape(NFREQ, 8, COLS).astype(BF16)
        for _, f in over_freq:
            c = remote(s2.at[f, o:o + size], b2.at[g, o:o + size], ss2.at[n, f], rs2.at[n, g], "freq", f)
            c.start()
            sends.append(c)
    for n, (o, size) in enumerate(PARTS):
        total = s2[g, o:o + size].astype(F32)
        for _, f in over_freq:
            dst = b2.at[f, o:o + size]
            remote(dst, dst, ss2.at[n, f], rs2.at[n, f], "freq", f).wait_recv()
            total = total + b2[f, o:o + size].astype(F32)
        s3[o:o + size] = total.astype(BF16)
        for _, kk in over_tile:
            c = remote(s3.at[o:o + size], b3.at[k, o:o + size], ss3.at[n, kk], rs3.at[n, k], "tile", kk)
            c.start()
            sends.append(c)
    b3[k] = s3[...]

    def table(kk):
        for p in range(CHUNK):
            x = b3[kk, p].astype(F32)
            xr, xi = x[0:4], x[4:8]
            x_ref[chunk_start(kk) + p] = jnp.concatenate([xr, xi - xr, xr + xi, xr], axis=0)

    table(k)
    for _, kk in over_tile[::-1]:
        for n, (o, size) in enumerate(PARTS):
            dst = b3.at[kk, o:o + size]
            remote(dst, dst, ss3.at[n, kk], rs3.at[n, kk], "tile", kk).wait_recv()
        table(kk)
    for c in sends:
        c.wait_send()


def project(v_ref, x_ref, rank_row, ct):
    row = lax.broadcasted_iota(jnp.int32, (8, COLS), 0)
    for h in range(2):
        def body(p, acc):
            acc = list(acc)
            for a in range(2):
                r = 16 * h + 8 * a
                re = v_ref[0, p, r:r + 8, :].astype(F32)
                im = v_ref[1, p, r:r + 8, :].astype(F32)
                for n, b in enumerate((re + im, re, im)):
                    for v in range(NV):
                        m = 4 * n + v
                        acc[12 * a + m] += b * jnp.broadcast_to(x_ref[p, m:m + 1, :COLS], (8, COLS))
            return tuple(acc)

        acc = lax.fori_loop(0, EXT, body, (jnp.zeros((8, COLS), F32),) * 24, unroll=35)
        for a in range(2):
            keep = row + (16 * h + 8 * a) < rank_row
            for v in range(NV):
                k1, k2, k3 = (acc[12 * a + 4 * n + v] for n in range(3))
                re = jnp.where(keep, k1 - k3, 0.0).astype(BF16)
                im = jnp.where(keep, k1 + k2, 0.0).astype(BF16)
                n = 128 * h + 64 * a + 16 * v
                ct[n:n + 8, 0:COLS] = re
                ct[n:n + 8, 128:128 + COLS] = -im
                ct[n + 8:n + 16, 0:COLS] = im
                ct[n + 8:n + 16, 128:128 + COLS] = re


def expand(u_ref, ct, diag):
    low = iota((EXT, 8, 128), 2) < 64
    us = [jnp.pad(u_ref[c].reshape(EXT * RANK, COLS), ((0, 0), (0, 128 - COLS))) for c in range(2)]
    z = lax.dot_general(jnp.concatenate(us, axis=1), ct[...], NT_DIMS, preferred_element_type=F32)
    z = z.reshape(EXT, 4, 8, 256)
    for h in range(2):
        lanes = slice(128 * h, 128 * h + 128)
        diag[h] = jnp.where(low, z[:, 2 * h, :, lanes], z[:, 2 * h + 1, :, lanes]).reshape(EXT * 8, 128)


def collect(diag):
    lane = lax.broadcasted_iota(jnp.int32, (EXT, 128), 1) % 8
    halves = []
    for h in range(2):
        tot = diag[h, pl.ds(0, EXT, stride=8), :]
        for b in range(1, 8):
            tot = jnp.where(lane == b, diag[h, pl.ds(b, EXT, stride=8), :], tot)
        halves.append(tot)
    hi, lo = split(jnp.concatenate(halves, axis=1))
    rows = lax.broadcasted_iota(jnp.int32, (8, 256), 0)
    lanes = lax.broadcasted_iota(jnp.int32, (8, 256), 1)
    pick = ((lanes % 64) // 8 == (rows % 4) * 2 + rows // 4).astype(BF16)
    dot = functools.partial(lax.dot_general, dimension_numbers=NT_DIMS, preferred_element_type=F32)
    return dot(pick, hi) + dot(pick, lo)


def apply_kernel(
    freq_ref, slab_ref, t_ref, rank_ref, v_hbm, u_hbm, b2,
    v_all, u_all, x_ref, w_ref, ct, diag, inv, ring, s1, b1, s2, vs, us, ss1, rs1, ss2, rs2, own, *scratch
):
    i = pl.program_id(0)
    g, k, over_tile, over_freq = peers()
    barrier = pltpu.get_barrier_semaphore()

    @pl.when(i == 0)
    def _():
        for _, kk in over_tile:
            pl.semaphore_signal(barrier, inc=1, device_id={"tile": kk}, device_id_type=MESH)
        for _, f in over_freq:
            pl.semaphore_signal(barrier, inc=1, device_id={"freq": f}, device_id_type=MESH)
        for n in range(ROWS):
            pltpu.make_async_copy(v_hbm.at[n], v_all.at[n], vs.at[n]).start()
            pltpu.make_async_copy(u_hbm.at[n], u_all.at[n], us.at[n]).start()
        ct[...] = jnp.zeros_like(ct)
        diag[...] = jnp.zeros_like(diag)

        def mats():
            w_ref[...] = forward_matrix(freq_ref, slab_ref, g)
            inv[...] = inverse_matrix(freq_ref, slab_ref, g)

        pl.semaphore_wait(barrier, NTILE + NFREQ - 2)
        spectra(g, k, over_tile, over_freq, mats, t_ref, x_ref, w_ref, *scratch)

    pltpu.make_async_copy(v_hbm.at[i], v_all.at[i], vs.at[i]).wait()
    project(v_all.at[i], x_ref, rank_ref[i], ct)
    pltpu.make_async_copy(u_hbm.at[i], u_all.at[i], us.at[i]).wait()

    def place(n, piece):
        start = (k * ROWS + n) * EXT
        off = lax.rem(start, 128)
        piece = pltpu.roll(jnp.pad(piece, ((0, 0), (0, 128 - EXT))), off, 1)
        head = iota((8, 128), 1) >= off
        odd = lax.rem(lax.div(start, 128), 2) == 1
        for t in range(2):
            before = jnp.where(lax.rem(n, BATCH) == 0, 0.0, ring[t])
            ring[t] = before + jnp.where(head == (odd if t else jnp.logical_not(odd)), piece, 0.0)

    def send(n):
        s1[n] = jnp.concatenate([ring[0], ring[1]], axis=1).astype(BF16)
        for _, f in over_freq:
            remote(s1.at[n], b1.at[n, g], ss1.at[f], rs1.at[n, g], "freq", f).start()
        b1[n, g] = s1[n]

    def finish(n):
        for _, f in over_freq:
            remote(s1.at[n], b1.at[n, f], ss1.at[f], rs1.at[n, f], "freq", f).wait_recv()
        r = b1[n].reshape(64, 256)
        res = jnp.dot(inv[...], jnp.concatenate([r, r], axis=0), preferred_element_type=F32)
        s2[:, n] = res.reshape(NTILE, 16, 256).astype(BF16)
        for _, kk in over_tile:
            remote(s2.at[kk, n], b2.at[k, n], ss2.at[kk], rs2.at[k], "tile", kk).start()
        pltpu.make_async_copy(s2.at[k, n], b2.at[k, n], own.at[n]).start()

    last = collect(diag)
    expand(u_all.at[i], ct, diag)
    place(jnp.maximum(i - 1, 0), last)

    @pl.when(jnp.logical_and(lax.rem(i, BATCH) == 0, i > 0))
    def _():
        send(lax.div(i, BATCH) - 1)

    @pl.when(jnp.logical_and(lax.rem(i, BATCH) == 0, i > BATCH))
    def _():
        finish(lax.div(i, BATCH) - 2)

    @pl.when(i == ROWS - 1)
    def _():
        place(i, collect(diag))
        send(NB - 1)
        finish(NB - 2)
        finish(NB - 1)
        for _, kk in over_tile:
            remote(s2.at[kk], b2.at[kk], ss2.at[kk], rs2.at[kk], "tile", kk).wait_recv()
        for n in range(NB):
            pltpu.make_async_copy(s2.at[k, n], b2.at[k, n], own.at[n]).wait()
        for _, f in over_freq:
            remote(s1, b1.at[:, f], ss1.at[f], rs1.at[0, f], "freq", f).wait_send()
        for _, kk in over_tile:
            remote(s2.at[kk], b2.at[kk], ss2.at[kk], rs2.at[kk], "tile", kk).wait_send()


def apply(freq_bin, slab_order, t, ranks, v, u):
    dma = pltpu.SemaphoreType.DMA
    smem = pl.BlockSpec(memory_space=pltpu.SMEM)
    vmem = pl.BlockSpec(memory_space=pltpu.VMEM)
    hbm = pl.BlockSpec(memory_space=pl.ANY)
    return pl.pallas_call(
        apply_kernel,
        grid=(ROWS,),
        out_shape=jax.ShapeDtypeStruct((NTILE, NB, 16, 256), BF16),
        in_specs=[smem, smem, vmem, vmem, hbm, hbm],
        out_specs=hbm,
        scratch_shapes=[
            pltpu.VMEM((ROWS, 2, EXT, RANK, COLS), BF16),
            pltpu.VMEM((ROWS, 2, EXT, RANK, COLS), BF16),
            pltpu.VMEM((EXT, 16, COLS), F32),
            pltpu.VMEM((128, 256), BF16),
            pltpu.VMEM((256, 256), BF16),
            pltpu.VMEM((2, EXT * 8, 128), F32),
            pltpu.VMEM((256, 128), BF16),
            pltpu.VMEM((2, 8, 128), F32),
            pltpu.VMEM((NB, 8, 256), BF16),
            pltpu.VMEM((NB, NFREQ, 8, 256), BF16),
            pltpu.VMEM((NTILE, NB, 16, 256), BF16),
            dma((ROWS,)), dma((ROWS,)),
            dma((NFREQ,)), dma((NB, NFREQ)), dma((NTILE,)), dma((NTILE,)), dma((NB,)),
            pltpu.VMEM((NTILE, CHUNK, 16, COLS), BF16),
            pltpu.VMEM((NFREQ, CHUNK, 8, COLS), BF16),
            pltpu.VMEM((NFREQ, CHUNK, 8, COLS), BF16),
            pltpu.VMEM((CHUNK, 8, COLS), BF16),
            pltpu.VMEM((NTILE, CHUNK, 8, COLS), BF16),
            dma,
            *(dma((len(PARTS), n)) for n in (NTILE, NTILE, NFREQ, NFREQ, NTILE, NTILE)),
        ],
        compiler_params=pltpu.CompilerParams(collective_id=0, has_side_effects=True),
    )(freq_bin, slab_order, t, ranks, v, u)


def assemble_kernel(b_ref, out_ref):
    lane = iota((16, 128), 1)
    width = BATCH * EXT
    for m in range(OUT // 128):
        vals = []
        for row in range(128 * m // width, (128 * m + 127) // width + 1):
            val = b_ref[row // NB, row % NB, :, 128 * (m % 2):128 * (m % 2) + 128]
            lo, hi = row * width - 128 * m, (row + 1) * width - 128 * m
            if lo > 0:
                val = jnp.where(lane >= lo, val, jnp.zeros_like(val))
            if hi < 128:
                val = jnp.where(lane < hi, val, jnp.zeros_like(val))
            vals.append(val)
        val = tree(vals)
        for t in range(NT):
            out_ref[t, m] = val[NV * t:NV * t + NV]


def assemble(b):
    vmem = pl.BlockSpec(memory_space=pltpu.VMEM)
    return pl.pallas_call(
        assemble_kernel,
        out_shape=jax.ShapeDtypeStruct((NT, OUT // 128, NV, 128), BF16),
        in_specs=[vmem],
        out_specs=vmem,
    )(b)


def local(virtual_source_trace, v_bases, u_bases, ranks, freq_bin, slab_order):
    t = virtual_source_trace.reshape(NT, NV, COLS, EXT).transpose(3, 0, 1, 2).reshape(EXT, 16, COLS)
    v = v_bases[0].transpose(0, 2, 4, 3, 1)
    u = u_bases[0].transpose(0, 2, 4, 3, 1)
    out = assemble(apply(freq_bin, slab_order, t, ranks.reshape(ROWS, 1, COLS), v, u))
    return out.transpose(0, 2, 1, 3).reshape(NT, NV, OUT)


def solution(mesh):
    in_specs = (
        P(("freq", "tile"), None, None),
        P("freq", "tile", None, None, None, None),
        P("freq", "tile", None, None, None, None),
        P("freq", "tile", None),
        P(),
        P(),
    )
    out_specs = P(("freq", "tile"), None, None)
    return jax.shard_map(local, mesh=mesh, in_specs=in_specs, out_specs=out_specs, check_vma=False)
```
